256 devices in a mesh: grp: 2 (over core), seq: 16 (over y, x), tp: 8 (over z).
Axes of the slice: x: 4, y: 4, z: 8, core: 2. Of those that a mesh axis runs over, the one named last changes fastest.
Arguments:
- prompt: bfloat16 [16384, 8192], P(('grp', 'seq'), 'tp'), may hold values from -6 to 6
- w_kv: bfloat16 [8192, 2048], P(None, 'tp'), may hold values from -0.0625 to 0.0625
- block_owner: int32 [2048, 1], P(('grp', 'seq')), may hold values from 0 to 31, as said below
- block_row: int32 [2048], P(('grp', 'seq')), may hold values from 0 to 31, as said below
- queries: bfloat16 [1024, 4, 8192], P(('grp', 'seq'), None, 'tp'), may hold values from -150 to 150
- new_kv: bfloat16 [1024, 4, 2048], P(('grp', 'seq'), None, 'tp'), may hold values from -6 to 6
- cache_codes: bfloat16 [1024, 128, 2048], P(('grp', 'seq'), None, 'tp'), may hold values from -4 to 4
- cache_scales: float32 [1024, 8, 16], P(('grp', 'seq'), None, 'tp'), may hold values from 0.5 to 2
- lengths: int32 [1024], P(('grp', 'seq')), may hold values from 1 to 128, 65536 in all
- w_out: bfloat16 [8192, 8192], P('tp', 'seq'), may hold values from -0.5 to 0.5
Outputs:
- mixed: bfloat16 [4096, 8192], P(('grp', 'tp'), 'seq')
The draws below stay inside these ranges and needn't reach their ends.
Inputs may be any that keep to these rules, and one draw needn't show every extreme that they name: `block_owner`: the blocks come in aligned groups of 8 consecutive blocks that share one owner and one request; the groups of one prefill device all go to different owners, so a prefill device sends exactly 8 blocks to each owner it sends to. `block_row`: equal on all blocks of one aligned group of 8 blocks.
All inputs are finite; a program needn't handle non-finite values. No bound on the sum of `lengths` on one device may be relied on, other than what follows from the above.
Results may differ from the reference program's by a relative error of at most 0.014.
Values may be sent and summed in bfloat16 or wider, within the bound.
No kernel may reach another device: no remote copies, remote signals or barrier semaphores. Data moves between devices by JAX's collectives and lax.ppermute only.
A program may use at most 256 MiB of HBM per device.

```python
import math
import jax
import jax.numpy as jnp
import numpy as np
from jax import lax

D = 8192
HQ = 64
KVH = 8
HD = 128
NEW = 4
BLK = 8
CBLK = 16
ROWS_DEV = 32
CTX = 128
NB_DEV = 64
CAP = 8
PTOK = 16384
NBLK = 2048
ROWS = 1024
N_GRP = 2
N_SEQ = 16
N_TP = 8


def cache_first(key):
    return jax.random.truncated_normal(jax.random.fold_in(key, 71), -4.0, 4.0, (ROWS, 1, KVH * 2 * HD), jnp.float32)


def group_plan(key):
    senders = NBLK // NB_DEV
    per_sender = NB_DEV // CAP
    sender_keys = jax.random.split(jax.random.fold_in(key, 81), senders)
    picks = jax.vmap(lambda one_key: jax.random.permutation(one_key, senders))(sender_keys)[:, :per_sender]
    owner_of_group = picks.reshape(senders * per_sender).astype(jnp.int32)
    row_of_group = jax.random.randint(jax.random.fold_in(key, 82), (senders * per_sender,), 0, ROWS_DEV).astype(jnp.int32)
    return (jnp.repeat(owner_of_group, CAP), jnp.repeat(row_of_group, CAP))


def draw_block_owner(key, part):
    owner_of_block, row_of_block = group_plan(key)
    return owner_of_block.reshape(NBLK, 1).astype(jnp.int32)


def draw_block_row(key, part):
    owner_of_block, row_of_block = group_plan(key)
    return row_of_block.astype(jnp.int32)


def draw_cache_codes(key, part):
    first_codes = cache_first(key)
    later_codes = jax.random.truncated_normal(jax.random.fold_in(key, 72), -4.0, 4.0, (ROWS, CTX - 1, KVH * 2 * HD), jnp.float32)
    return jnp.concatenate([first_codes, later_codes], axis=1).astype(jnp.bfloat16)


def draw_queries(key, part):
    base_draw = jax.random.truncated_normal(jax.random.fold_in(key, 73), -6.0, 6.0, (ROWS, NEW, HQ * HD), jnp.float32)
    return base_draw.astype(jnp.bfloat16)


def steps_of(stream_key, shape, pieces, least, top_value):
    gain = 1.0
    for dim, shards_of in pieces:
        steps = jax.random.uniform(jax.random.fold_in(jax.random.fold_in(stream_key, 6), dim), (shards_of,), jnp.float32, least / len(pieces), top_value / len(pieces))
        gain = gain * jnp.repeat(jnp.exp(steps), shape[dim] // shards_of).reshape((-1,) + (1,) * (len(shape) - 1 - dim))
    return gain


def split_up(amount, total, most, slope):
    portions = [(1 << 20) // math.isqrt(standing ** slope) + 1 for standing in range(2, amount + 1)]
    spare, holding = total - most - (amount - 1), [1] * (amount - 1)
    while spare > 0:
        free = [i for i in range(amount - 1) if holding[i] < most]
        whole, budget = sum([portions[i] for i in free]), spare
        for i in free:
            more = min(most - holding[i], max(1, budget * portions[i] // whole), spare)
            holding[i] = holding[i] + more
            spare = spare - more
    return np.array([most] + holding)


def uneven(key, amount, total, bound, slope):
    if amount == 2:
        one = jax.random.randint(key, (), max(1, total - bound), min(bound, total - 1) + 1)
        return jnp.stack([one, total - one])
    sizes = jnp.asarray(split_up(amount, total, bound, slope), jnp.int32)
    twos = (amount - 1) // 2
    giver, sink = sizes[1:1 + 2 * twos:2], sizes[2:2 + 2 * twos:2]
    room = jnp.minimum(giver - 1, bound - sink)
    moved = jax.random.randint(jax.random.fold_in(key, 1), (twos,), 0, 1 << 20) % (room + 1)
    sizes = sizes.at[1:1 + 2 * twos:2].set(giver - moved).at[2:2 + 2 * twos:2].set(sink + moved)
    return sizes[jax.random.permutation(jax.random.fold_in(key, 2), amount)]


def gaussian(rng, dims, deviation, reach, shards=(), held_as=jnp.bfloat16):
    drawn = jax.random.normal(rng, dims, jnp.float32) * deviation
    if len(shards) > 0:
        drawn = steps_of(rng, dims, shards, -0.22, 0.18) * drawn
    return jnp.clip(drawn, min=-reach, max=reach).astype(held_as)


def setup_inputs(seed: int = 0) -> dict:
    streams_of = jax.random.split(jax.random.key(seed), 11)
    return {
        "prompt": gaussian(streams_of[0], (PTOK, D), 1.0, 6.0, ((0, 32), (1, 8))),
        "w_kv": gaussian(streams_of[1], (D, KVH * 2 * HD), D ** -0.5, 0.0625, ((1, 8),)),
        "block_owner": draw_block_owner(jax.random.fold_in(streams_of[10], 71), 0),
        "block_row": draw_block_row(jax.random.fold_in(streams_of[10], 71), 0),
        "queries": draw_queries(jax.random.fold_in(streams_of[10], 71), 0),
        "new_kv": gaussian(streams_of[5], (ROWS, NEW, KVH * 2 * HD), 1.0, 6.0, ((0, 32), (2, 8))),
        "cache_codes": draw_cache_codes(jax.random.fold_in(streams_of[10], 71), 0),
        "cache_scales": jnp.clip(jnp.exp(math.log(2.0) - 1.3862944 * jax.random.uniform(streams_of[7], (ROWS, CTX // CBLK, KVH * 2), jnp.float32) ** steps_of(streams_of[7], (ROWS, CTX // CBLK, KVH * 2), ((0, 32), (2, 8)), -0.2, 0.2)), 0.5, 2.0),
        "lengths": uneven(streams_of[8], ROWS, ROWS * CTX // 2, CTX, 2).astype(jnp.int32),
        "w_out": gaussian(streams_of[9], (HQ * HD, D), HD ** -0.5, 0.5, ((0, 8), (1, 16))),
    }


EPS = 1e-05

def rounded(values):
    return lax.optimization_barrier(values.astype(jnp.bfloat16)).astype(jnp.float32)

def reference(prompt, w_kv, block_owner, block_row, queries, new_kv, cache_codes, cache_scales, lengths, w_out):
    widened = prompt.astype(jnp.float32)
    row_scale = lax.rsqrt(lax.optimization_barrier(jnp.sum(widened * widened, axis=1)) / D + EPS)
    prompt_kv = (jnp.dot(prompt, w_kv, preferred_element_type=jnp.float32) * row_scale[:, None]).astype(jnp.bfloat16)
    dest_block = (block_owner[:, 0] * ROWS_DEV + block_row).astype(jnp.int32)
    dest_token = jnp.repeat(dest_block, BLK)
    head_group = HQ // KVH
    query_heads = queries.astype(jnp.float32).reshape(ROWS, NEW, KVH, head_group, HD)
    fresh_all = new_kv.reshape(ROWS, NEW, KVH, 2, HD)
    stored = cache_codes.reshape(ROWS, CTX, KVH, 2, HD)
    block_scales = cache_scales.reshape(ROWS, CTX // CBLK, KVH, 2)
    prompt_heads = prompt_kv.reshape(PTOK, KVH, 2, HD)
    inverse_root = 1.0 / math.sqrt(HD)
    owners = N_GRP * N_SEQ
    zero_index = jnp.zeros((), jnp.int32)

    def attend(pair_index):
        owner_id = pair_index // KVH
        head_id = pair_index % KVH
        first_row = (owner_id * ROWS_DEV).astype(jnp.int32)
        query_part = lax.dynamic_slice(query_heads, (first_row, zero_index, head_id, zero_index, zero_index), (ROWS_DEV, NEW, 1, head_group, HD))[:, :, 0]
        fresh_kv = lax.dynamic_slice(fresh_all, (first_row, zero_index, head_id, zero_index, zero_index), (ROWS_DEV, NEW, 1, 2, HD))[:, :, 0].astype(jnp.float32)
        stored_part = lax.dynamic_slice(stored, (first_row, zero_index, head_id, zero_index, zero_index), (ROWS_DEV, CTX, 1, 2, HD))[:, :, 0].astype(jnp.float32)
        scale_part = lax.dynamic_slice(block_scales, (first_row, zero_index, head_id, zero_index), (ROWS_DEV, CTX // CBLK, 1, 2))[:, :, 0]
        length_part = lax.dynamic_slice(lengths, (first_row,), (ROWS_DEV,))
        prompt_part = lax.dynamic_slice(prompt_heads, (zero_index, head_id, zero_index, zero_index), (PTOK, 1, 2, HD))[:, 0].astype(jnp.float32)
        key_scale = jnp.repeat(scale_part[:, :, 0], CBLK, axis=1)
        value_scale = jnp.repeat(scale_part[:, :, 1], CBLK, axis=1)
        row_ids = first_row + jnp.arange(ROWS_DEV, dtype=jnp.int32)
        s_cache = jnp.einsum('rihd,rpd->rihp', query_part, stored_part[:, :, 0]) * key_scale[:, None, None, :] * inverse_root
        cache_live = jnp.arange(CTX, dtype=jnp.int32)[None, :] < length_part[:, None]
        s_cache = jnp.where(cache_live[:, None, None, :], s_cache, -jnp.inf)
        s_sent = jnp.einsum('rihd,kd->rihk', query_part, prompt_part[:, 0]) * inverse_root
        sent_live = dest_token[None, :] == row_ids[:, None]
        s_sent = jnp.where(sent_live[:, None, None, :], s_sent, -jnp.inf)
        s_fresh = jnp.einsum('rihd,rjd->rihj', query_part, fresh_kv[:, :, 0]) * inverse_root
        causal = jnp.arange(NEW)[None, :] <= jnp.arange(NEW)[:, None]
        s_fresh = jnp.where(causal[None, :, None, :], s_fresh, -jnp.inf)
        row_max = jnp.maximum(jnp.maximum(lax.optimization_barrier(jnp.max(s_cache, axis=-1)), lax.optimization_barrier(jnp.max(s_sent, axis=-1))), lax.optimization_barrier(jnp.max(s_fresh, axis=-1)))
        w_cache = jnp.exp(s_cache - row_max[..., None])
        w_sent = jnp.exp(s_sent - row_max[..., None])
        w_fresh = jnp.exp(s_fresh - row_max[..., None])
        denominator = lax.optimization_barrier(jnp.sum(w_cache, axis=-1)) + lax.optimization_barrier(jnp.sum(w_sent, axis=-1)) + lax.optimization_barrier(jnp.sum(w_fresh, axis=-1))
        numerator = jnp.einsum('rihp,rpd->rihd', rounded(w_cache * value_scale[:, None, None, :]), stored_part[:, :, 1])
        numerator = numerator + jnp.einsum('rihk,kd->rihd', rounded(w_sent), prompt_part[:, 1])
        numerator = numerator + jnp.einsum('rihj,rjd->rihd', rounded(w_fresh), fresh_kv[:, :, 1])
        return (numerator / denominator[..., None]).astype(jnp.bfloat16)
    results = lax.map(attend, jnp.arange(owners * KVH, dtype=jnp.int32))
    results = results.reshape(owners, KVH, ROWS_DEV, NEW, head_group, HD)
    attention = jnp.transpose(results, (0, 2, 3, 1, 4, 5)).reshape(ROWS * NEW, HQ * HD)
    per_group = HQ * HD // N_TP
    mixed = jnp.zeros((ROWS * NEW, D), jnp.float32)
    for group_id in range(N_TP):
        group_term = jnp.dot(attention[:, group_id * per_group:(group_id + 1) * per_group], w_out[group_id * per_group:(group_id + 1) * per_group], preferred_element_type=jnp.float32)
        mixed = mixed + rounded(group_term)
    return mixed.astype(jnp.bfloat16)
```

```python
import math

import jax
import jax.numpy as jnp
from jax import lax
from jax.experimental import pallas as pl
from jax.experimental.pallas import tpu as pltpu
from jax.sharding import PartitionSpec as P

HQ = 64
KVH = 8
HD = 128
NEW = 4
BLK = 8
CBLK = 16
CAP = 8
EPS = 1e-05
INV_ROOT = 1.0 / math.sqrt(HD)
F32 = jnp.float32
BF16 = jnp.bfloat16


def shift_tp(x, k):
    n = lax.axis_size("tp")
    return lax.ppermute(x, "tp", [(i, (i + k) % n) for i in range(n)])


def pack_kernel(idx_ref, run_ref, sq_ref, out_ref, kv_ref, *, features):
    scale = lax.rsqrt(sq_ref[...] / features + EPS)
    kv_ref[...] = (run_ref[...] * scale).astype(BF16).reshape(kv_ref.shape)
    for o in range(out_ref.shape[0]):
        out_ref[o] = kv_ref[idx_ref[o]]


def pack(idx, run, sq, owners, groups, features):
    tokens, columns = run.shape
    return pl.pallas_call(
        lambda *refs: pack_kernel(*refs, features=features),
        out_shape=jax.ShapeDtypeStruct((owners, tokens // groups, columns), BF16),
        in_specs=[
            pl.BlockSpec(memory_space=pltpu.SMEM),
            pl.BlockSpec(memory_space=pltpu.VMEM),
            pl.BlockSpec(memory_space=pltpu.VMEM),
        ],
        out_specs=pl.BlockSpec(memory_space=pltpu.VMEM),
        scratch_shapes=[pltpu.VMEM((groups, tokens // groups, columns), BF16)],
        name="pack_kv",
    )(idx, run, sq)


def sent_kernel(rows_ref, q_ref, kv_ref, m_ref, l_ref, a_ref, out_ref, m_s, l_s, a_s, m_k, l_k, a_k):
    m_s[...] = m_ref[...]
    l_s[...] = l_ref[...]
    a_s[...] = a_ref[...]
    slots = kv_ref.shape[0]
    for k in range(slots):
        row = jnp.maximum(rows_ref[k], 0)
        s = (
            lax.dot_general(
                q_ref[row], kv_ref[k, :, :HD], (((1,), (1,)), ((), ())), preferred_element_type=F32
            )
            * INV_ROOT
        )
        top = jnp.max(s, axis=1, keepdims=True)
        w = jnp.exp(s - top)
        m_k[k] = jnp.broadcast_to(top, m_k.shape[1:])
        l_k[k] = jnp.broadcast_to(jnp.sum(w, axis=1, keepdims=True), l_k.shape[1:])
        a_k[k] = jnp.dot(w.astype(BF16), kv_ref[k, :, HD:], preferred_element_type=F32)
    for k in range(slots):
        row = rows_ref[k]

        @pl.when(row >= 0)
        def _():
            old, new = m_s[row], m_k[k]
            top = jnp.maximum(old, new)
            keep, fresh = jnp.exp(old - top), jnp.exp(new - top)
            m_s[row] = top
            l_s[row] = l_s[row] * keep + l_k[k] * fresh
            a_s[row] = a_s[row] * keep + a_k[k] * fresh

    out_ref[...] = (a_s[...] / l_s[...]).astype(BF16)


def sent_attention(rows, q, kv, m, l, acc):
    slots = kv.shape[0]
    vm = pl.BlockSpec(memory_space=pltpu.VMEM)
    state = pltpu.VMEM(acc.shape, F32)
    per_slot = pltpu.VMEM((slots,) + acc.shape[1:], F32)
    return pl.pallas_call(
        sent_kernel,
        out_shape=jax.ShapeDtypeStruct(q.shape, BF16),
        in_specs=[pl.BlockSpec(memory_space=pltpu.SMEM), vm, vm, vm, vm, vm],
        out_specs=vm,
        scratch_shapes=[state, state, state, per_slot, per_slot, per_slot],
        name="sent_attention",
    )(rows, q, kv, m, l, acc)


def own_attention(q, new_kv, cache_codes, cache_scales, lengths):
    rows, context = cache_codes.shape[:2]
    group = q.shape[1] // NEW
    key_scale = jnp.repeat(cache_scales[:, :, 0], CBLK, axis=1)
    value_scale = jnp.repeat(cache_scales[:, :, 1], CBLK, axis=1)
    s_cache = jnp.einsum("rqd,rpd->rqp", q, cache_codes[:, :, :HD], preferred_element_type=F32)
    s_cache = s_cache * key_scale[:, None, :] * INV_ROOT
    live = jnp.arange(context, dtype=jnp.int32)[None, :] < lengths[:, None]
    s_cache = jnp.where(live[:, None, :], s_cache, -jnp.inf)
    s_new = jnp.einsum("rqd,rjd->rqj", q, new_kv[:, :, :HD], preferred_element_type=F32) * INV_ROOT
    causal = jnp.arange(NEW)[None, :] <= (jnp.arange(NEW * group) // group)[:, None]
    s_new = jnp.where(causal[None], s_new, -jnp.inf)
    m = jnp.maximum(jnp.max(s_cache, axis=-1), jnp.max(s_new, axis=-1))
    w_cache = jnp.exp(s_cache - m[..., None])
    w_new = jnp.exp(s_new - m[..., None])
    l = jnp.sum(w_cache, axis=-1) + jnp.sum(w_new, axis=-1)
    acc = jnp.einsum(
        "rqp,rpd->rqd",
        (w_cache * value_scale[:, None, :]).astype(BF16),
        cache_codes[:, :, HD:],
        preferred_element_type=F32,
    ) + jnp.einsum(
        "rqj,rjd->rqd", w_new.astype(BF16), new_kv[:, :, HD:], preferred_element_type=F32
    )
    wide = acc.shape
    return jnp.broadcast_to(m[..., None], wide), jnp.broadcast_to(l[..., None], wide), acc


def project(prompt, w_kv):
    n = lax.axis_size("tp")
    me = lax.axis_index("tp")
    tokens, part = prompt.shape
    blocks = w_kv.reshape(n, part, w_kv.shape[1])
    half = tokens // 2

    def term(piece, k):
        w = lax.dynamic_index_in_dim(blocks, (me + k) % n, 0, keepdims=False)
        wide = piece.astype(F32)
        return (
            jnp.dot(piece, w, preferred_element_type=F32),
            jnp.sum(wide * wide, axis=1, keepdims=True),
        )

    pieces = [prompt[:half], prompt[half:]]
    up, down = list(pieces), list(pieces)
    sums = [term(p, 0) for p in pieces]

    def add(c, piece, k):
        run, sq = term(piece, k)
        sums[c] = (sums[c][0] + run, sums[c][1] + sq)

    for step in range(1, n // 2):
        for c in range(2):
            up[c], down[c] = shift_tp(up[c], 1), shift_tp(down[c], -1)
        for c in range(2):
            add(c, up[c], -step)
            add(c, down[c], step)
    up[0], down[1] = shift_tp(up[0], 1), shift_tp(down[1], -1)
    add(0, up[0], n // 2)
    add(1, down[1], n // 2)
    return (
        jnp.concatenate([sums[0][0], sums[1][0]], axis=0),
        jnp.concatenate([sums[0][1], sums[1][1]], axis=0),
    )


def on_device(
    prompt, w_kv, block_owner, block_row, queries, new_kv, cache_codes, cache_scales, lengths, w_out
):
    owners = lax.axis_size("grp") * lax.axis_size("seq")
    row_count = queries.shape[0]
    head_group = HQ // KVH
    features = w_kv.shape[0]
    groups = block_row.shape[0] // CAP

    group_owner, group_row = block_owner[::CAP, 0], block_row[::CAP]
    hit = group_owner[None, :] == jnp.arange(owners, dtype=jnp.int32)[:, None]
    idx = jnp.sum(jnp.where(hit, jnp.arange(groups, dtype=jnp.int32)[None, :], 0), axis=1)
    send_rows = jnp.sum(jnp.where(hit, group_row[None, :] + 1, 0), axis=1) - 1
    rows = lax.all_to_all(
        jnp.broadcast_to(send_rows[:, None], (owners, 8)), ("grp", "seq"), 0, 0, tiled=True
    )[:, 0]

    q = queries.reshape(row_count, NEW * head_group, HD)
    m, l, acc = own_attention(q, new_kv, cache_codes, cache_scales, lengths)

    run, sq = project(prompt, w_kv)
    send_kv = pack(idx, run, sq, owners, groups, features)
    kv = lax.all_to_all(send_kv, ("grp", "seq"), 0, 0, tiled=True)
    attention = sent_attention(rows, q, kv, m, l, acc).reshape(row_count * NEW, head_group * HD)
    head_terms = jnp.dot(
        lax.all_gather(attention, "seq", axis=0, tiled=True), w_out, preferred_element_type=F32
    )
    return lax.psum_scatter(head_terms.astype(BF16), "tp", scatter_dimension=0, tiled=True)


def solution(mesh):
    owner = ("grp", "seq")
    in_specs = (
        P(owner, "tp"),
        P(None, "tp"),
        P(owner, None),
        P(owner),
        P(owner, None, "tp"),
        P(owner, None, "tp"),
        P(owner, None, "tp"),
        P(owner, None, "tp"),
        P(owner),
        P("tp", "seq"),
    )
    out_specs = P(("grp", "tp"), "seq")
    return jax.shard_map(
        on_device, mesh=mesh, in_specs=in_specs, out_specs=out_specs, check_vma=False
    )
```

```python
import math

import jax
import jax.numpy as jnp
from jax import lax
from jax.experimental import pallas as pl
from jax.experimental.pallas import tpu as pltpu
from jax.sharding import PartitionSpec as P

HQ = 64
KVH = 8
HD = 128
NEW = 4
BLK = 8
CBLK = 16
CAP = 8
WAYS = 4
EPS = 1e-05
INV_ROOT = 1.0 / math.sqrt(HD)
F32 = jnp.float32
BF16 = jnp.bfloat16


def shift_tp(x, k):
    n = lax.axis_size("tp")
    return lax.ppermute(x, "tp", [(i, (i + k) % n) for i in range(n)])


def pack_kernel(idx_ref, run_ref, sq_ref, out_ref, kv_ref, *, features):
    scale = lax.rsqrt(sq_ref[...] / features + EPS)
    kv_ref[...] = (run_ref[...] * scale).astype(BF16).reshape(kv_ref.shape)
    for o in range(out_ref.shape[0]):
        out_ref[o] = kv_ref[idx_ref[o]]


def pack(idx, run, sq, owners, groups, features):
    tokens, columns = run.shape
    return pl.pallas_call(
        lambda *refs: pack_kernel(*refs, features=features),
        out_shape=jax.ShapeDtypeStruct((owners, tokens // groups, columns), BF16),
        in_specs=[
            pl.BlockSpec(memory_space=pltpu.SMEM),
            pl.BlockSpec(memory_space=pltpu.VMEM),
            pl.BlockSpec(memory_space=pltpu.VMEM),
        ],
        out_specs=pl.BlockSpec(memory_space=pltpu.VMEM),
        scratch_shapes=[pltpu.VMEM((groups, tokens // groups, columns), BF16)],
        name="pack_kv",
    )(idx, run, sq)


def sent_kernel(
    rows_ref, q_ref, kv_ref, m_ref, l_ref, a_ref, out_ref, order_ref, m_s, l_s, a_s, wide_ref
):
    slots = kv_ref.shape[0]
    requests = q_ref.shape[0]
    for k in range(slots + WAYS):
        order_ref[k] = 0
    count = 0
    for k in range(slots):
        order_ref[count] = k
        count = count + jnp.where(rows_ref[k] >= 0, 1, 0)
    m_s[...] = m_ref[...]
    l_s[...] = l_ref[...]
    a_s[...] = a_ref[...]

    def some_slots(j, carry):
        found = []
        for u in range(WAYS):
            at = j * WAYS + u
            k = order_ref[at]
            row = jnp.maximum(rows_ref[k], 0)
            s = (
                lax.dot_general(
                    q_ref[row],
                    kv_ref[k, :, :HD],
                    (((1,), (1,)), ((), ())),
                    preferred_element_type=F32,
                )
                * INV_ROOT
            )
            top = jnp.max(s, axis=1, keepdims=True)
            w = jnp.exp(s - top)
            total = jnp.sum(w, axis=1, keepdims=True)
            acc = jnp.dot(w.astype(BF16), kv_ref[k, :, HD:], preferred_element_type=F32)
            found.append((row, jnp.where(at < count, top, -jnp.inf), total, acc))
        for row, new, total, acc in found:
            old = m_s[row]
            top = jnp.maximum(old, new)
            keep, fresh = jnp.exp(old - top), jnp.exp(new - top)
            m_s[row] = top
            l_s[row] = l_s[row] * keep + total * fresh
            a_s[row] = a_s[row] * keep + acc * fresh
        return carry

    lax.fori_loop(0, (count + WAYS - 1) // WAYS, some_slots, 0)
    for r in range(requests):
        value = a_s[r] / l_s[r]
        for h in range(value.shape[0] // NEW):
            wide_ref[r * NEW : (r + 1) * NEW, h * HD : (h + 1) * HD] = value[h * NEW : (h + 1) * NEW]
    value = wide_ref[...].astype(BF16)
    for c in range(out_ref.shape[0]):
        out_ref[c] = value


def sent_attention(rows, q, kv, m, l, acc, copies):
    slots = kv.shape[0]
    vm = pl.BlockSpec(memory_space=pltpu.VMEM)
    state = pltpu.VMEM(acc.shape, F32)
    wide = (q.shape[0] * NEW, q.shape[1] // NEW * HD)
    return pl.pallas_call(
        sent_kernel,
        out_shape=jax.ShapeDtypeStruct((copies,) + wide, BF16),
        in_specs=[pl.BlockSpec(memory_space=pltpu.SMEM), vm, vm, vm, vm, vm],
        out_specs=vm,
        scratch_shapes=[
            pltpu.SMEM((slots + WAYS,), jnp.int32),
            state,
            state,
            state,
            pltpu.VMEM(wide, F32),
        ],
        name="sent_attention",
    )(rows, q, kv, m, l, acc)


def terms_kernel(where_ref, g_ref, w_ref, *outs, steps, planes):
    plane, column, core = where_ref[0], where_ref[1], where_ref[2]
    columns, half = w_ref.shape[1], w_ref.shape[2]
    width = w_ref.shape[3]
    for k, out_ref in zip(steps, outs, strict=True):
        dest = lax.rem(plane + k, planes)
        rows, side = dest // 2, lax.rem(dest, 2)
        for i in range(2):
            d = lax.rem(2 * side + i - column + columns, columns)
            total = jnp.dot(g_ref[rows, :, :half], w_ref[core, d], preferred_element_type=F32)
            total += jnp.dot(g_ref[rows, :, half:], w_ref[1 - core, d], preferred_element_type=F32)
            out_ref[:, i * width : (i + 1) * width] = total.astype(BF16)


def terms(where, gathered, w, steps, planes):
    vm = pl.BlockSpec(memory_space=pltpu.VMEM)
    shape = jax.ShapeDtypeStruct((gathered.shape[1], 2 * w.shape[3]), BF16)
    return pl.pallas_call(
        lambda *refs: terms_kernel(*refs, steps=steps, planes=planes),
        out_shape=[shape] * len(steps),
        in_specs=[pl.BlockSpec(memory_space=pltpu.SMEM), vm, vm],
        out_specs=[vm] * len(steps),
        name="out_terms",
    )(where, gathered, w)


def shift_x(v, k):
    n = lax.axis_size("x")
    return lax.ppermute(v, "x", [(i, (i + k) % n) for i in range(n)])


def gather_w_out(w_out):
    core = lax.axis_index("grp")
    half = w_out.shape[0] // 2
    own = lax.dynamic_index_in_dim(w_out.reshape(2, half, -1), core, 0, keepdims=False)
    before, after = shift_x(own, 1), shift_x(own, -1)
    far_a, far_b = shift_x(before[: half // 2], 1), shift_x(after[half // 2 :], -1)
    mine = jnp.stack([own, after, jnp.concatenate([far_a, far_b], axis=0), before])
    other = lax.ppermute(mine, "grp", [(0, 1), (1, 0)])
    return jnp.stack([mine, other])


def add_rounded(a, b):
    return (a.astype(F32) + b.astype(F32)).astype(BF16)


def mix(gathered, w):
    planes = lax.axis_size("tp")
    me, x, core = lax.axis_index("tp"), lax.axis_index("x"), lax.axis_index("grp")
    where = jnp.stack([me, x, core]).astype(jnp.int32)
    far = planes // 2
    (first,) = terms(where, gathered, w, (far,), planes)
    half = first.shape[0] // 2
    up, down = shift_tp(first[:half], 1), shift_tp(first[half:], -1)
    steps = [k for k in range(planes) if k != far]
    part = dict(zip(steps, terms(where, gathered, w, tuple(steps), planes), strict=True))
    near, back = part[far - 1], part[far + 1]
    up = shift_tp(jnp.concatenate([add_rounded(near[:half], up), near[half:]], axis=0), 1)
    down = shift_tp(jnp.concatenate([back[:half], add_rounded(back[half:], down)], axis=0), -1)
    for k in range(far - 2, 0, -1):
        up, down = (
            shift_tp(add_rounded(part[k], up), 1),
            shift_tp(add_rounded(part[planes - k], down), -1),
        )
    done = (part[0].astype(F32) + up.astype(F32) + down.astype(F32)).astype(BF16)
    width = done.shape[1] // 2
    xs, per = lax.axis_size("x"), lax.axis_size("x") * planes
    got = []
    for k in range(2):
        moves = []
        for xo in range(xs):
            for t in range(planes):
                to = (2 * (t % 2) + ((xo % 2) ^ k)) * planes + 2 * (t // 2) + xo // 2
                moves.append((xo * planes + t, to))
        piece = jnp.where(x % 2 == k, done[:, :width], done[:, width:])
        got.append(lax.ppermute(piece, ("x", "tp"), moves))
    return jnp.where(
        x % 2 == 0, jnp.concatenate([got[0], got[1]], axis=0), jnp.concatenate([got[1], got[0]], axis=0)
    )


def own_attention(q, new_kv, cache_codes, cache_scales, lengths):
    rows, context = cache_codes.shape[:2]
    group = q.shape[1] // NEW
    key_scale = jnp.repeat(cache_scales[:, :, 0], CBLK, axis=1)
    value_scale = jnp.repeat(cache_scales[:, :, 1], CBLK, axis=1)
    s_cache = jnp.einsum("rqd,rpd->rqp", q, cache_codes[:, :, :HD], preferred_element_type=F32)
    s_cache = s_cache * key_scale[:, None, :] * INV_ROOT
    live = jnp.arange(context, dtype=jnp.int32)[None, :] < lengths[:, None]
    s_cache = jnp.where(live[:, None, :], s_cache, -jnp.inf)
    s_new = jnp.einsum("rqd,rjd->rqj", q, new_kv[:, :, :HD], preferred_element_type=F32) * INV_ROOT
    causal = jnp.arange(NEW)[None, :] <= (jnp.arange(NEW * group) % NEW)[:, None]
    s_new = jnp.where(causal[None], s_new, -jnp.inf)
    m = jnp.maximum(jnp.max(s_cache, axis=-1), jnp.max(s_new, axis=-1))
    w_cache = jnp.exp(s_cache - m[..., None])
    w_new = jnp.exp(s_new - m[..., None])
    l = jnp.sum(w_cache, axis=-1) + jnp.sum(w_new, axis=-1)
    acc = jnp.einsum(
        "rqp,rpd->rqd",
        (w_cache * value_scale[:, None, :]).astype(BF16),
        cache_codes[:, :, HD:],
        preferred_element_type=F32,
    ) + jnp.einsum(
        "rqj,rjd->rqd", w_new.astype(BF16), new_kv[:, :, HD:], preferred_element_type=F32
    )
    wide = acc.shape
    return jnp.broadcast_to(m[..., None], wide), jnp.broadcast_to(l[..., None], wide), acc


def project(prompt, w_kv):
    n = lax.axis_size("tp")
    me = lax.axis_index("tp")
    tokens, part = prompt.shape
    blocks = w_kv.reshape(n, part, w_kv.shape[1])
    half = tokens // 2

    def term(piece, k):
        w = lax.dynamic_index_in_dim(blocks, (me + k) % n, 0, keepdims=False)
        wide = piece.astype(F32)
        return (
            jnp.dot(piece, w, preferred_element_type=F32),
            jnp.sum(wide * wide, axis=1, keepdims=True),
        )

    pieces = [prompt[:half], prompt[half:]]
    up, down = list(pieces), list(pieces)
    sums = [term(p, 0) for p in pieces]

    def add(c, piece, k):
        run, sq = term(piece, k)
        sums[c] = (sums[c][0] + run, sums[c][1] + sq)

    for step in range(1, n // 2):
        for c in range(2):
            up[c], down[c] = shift_tp(up[c], 1), shift_tp(down[c], -1)
        for c in range(2):
            add(c, up[c], -step)
            add(c, down[c], step)
    up[0], down[1] = shift_tp(up[0], 1), shift_tp(down[1], -1)
    add(0, up[0], n // 2)
    add(1, down[1], n // 2)
    return (
        jnp.concatenate([sums[0][0], sums[1][0]], axis=0),
        jnp.concatenate([sums[0][1], sums[1][1]], axis=0),
    )


def on_device(
    prompt, w_kv, block_owner, block_row, queries, new_kv, cache_codes, cache_scales, lengths, w_out
):
    owners = lax.axis_size("grp") * lax.axis_size("y") * lax.axis_size("x")
    row_count = queries.shape[0]
    head_group = HQ // KVH
    features = w_kv.shape[0]
    groups = block_row.shape[0] // CAP

    group_owner, group_row = block_owner[::CAP, 0], block_row[::CAP]
    hit = group_owner[None, :] == jnp.arange(owners, dtype=jnp.int32)[:, None]
    idx = jnp.sum(jnp.where(hit, jnp.arange(groups, dtype=jnp.int32)[None, :], 0), axis=1)
    send_rows = jnp.sum(jnp.where(hit, group_row[None, :] + 1, 0), axis=1) - 1
    rows = lax.all_to_all(
        jnp.broadcast_to(send_rows[:, None], (owners, 8)), ("grp", "y", "x"), 0, 0, tiled=True
    )[:, 0]

    q = queries.reshape(row_count, NEW, head_group, HD).transpose(0, 2, 1, 3)
    q = q.reshape(row_count, head_group * NEW, HD)
    m, l, acc = own_attention(q, new_kv, cache_codes, cache_scales, lengths)

    w = gather_w_out(w_out)
    run, sq = project(prompt, w_kv)
    send_kv = pack(idx, run, sq, owners, groups, features)
    kv = lax.all_to_all(send_kv, ("grp", "y", "x"), 0, 0, tiled=True)
    attention = sent_attention(rows, q, kv, m, l, acc, lax.axis_size("y"))
    gathered = lax.all_to_all(attention, "y", 0, 0, tiled=True)
    return mix(gathered, w)


def solution(mesh):
    side = math.isqrt(mesh.shape["seq"])
    sizes = (mesh.shape["grp"], side, side, mesh.shape["tp"])
    mesh = jax.sharding.Mesh(mesh.devices.reshape(sizes), ("grp", "y", "x", "tp"))
    owner = ("grp", "y", "x")
    in_specs = (
        P(owner, "tp"),
        P(None, "tp"),
        P(owner, None),
        P(owner),
        P(owner, None, "tp"),
        P(owner, None, "tp"),
        P(owner, None, "tp"),
        P(owner, None, "tp"),
        P(owner),
        P("tp", ("y", "x")),
    )
    out_specs = P(("grp", "tp"), ("y", "x"))
    return jax.shard_map(
        on_device, mesh=mesh, in_specs=in_specs, out_specs=out_specs, check_vma=False
    )
```

```python
import math

import jax
import jax.numpy as jnp
from jax import lax
from jax.experimental import pallas as pl
from jax.experimental.pallas import tpu as pltpu
from jax.sharding import PartitionSpec as P

HQ = 64
KVH = 8
HD = 128
NEW = 4
BLK = 8
CBLK = 16
CAP = 8
WAYS = 4
EPS = 1e-05
INV_ROOT = 1.0 / math.sqrt(HD)
F32 = jnp.float32
BF16 = jnp.bfloat16


def shift_tp(x, k):
    n = lax.axis_size("tp")
    return lax.ppermute(x, "tp", [(i, (i + k) % n) for i in range(n)])


def pack_kernel(idx_ref, run_a, run_b, sq_a, sq_b, out_ref, kv_ref, *, features):
    part = kv_ref.shape[0] // 2
    for c, (run, sq) in enumerate(((run_a, sq_a), (run_b, sq_b))):
        scale = lax.rsqrt(sq[...] / features + EPS)
        value = (run[...] * scale).astype(BF16)
        kv_ref[c * part : (c + 1) * part] = value.reshape((part,) + kv_ref.shape[1:])
    for o in range(out_ref.shape[0]):
        out_ref[o] = kv_ref[idx_ref[o]]


def pack(idx, sums, owners, groups, features):
    (run_a, sq_a), (run_b, sq_b) = sums
    tokens, columns = 2 * run_a.shape[0], run_a.shape[1]
    vm = pl.BlockSpec(memory_space=pltpu.VMEM)
    return pl.pallas_call(
        lambda *refs: pack_kernel(*refs, features=features),
        out_shape=jax.ShapeDtypeStruct((owners, tokens // groups, columns), BF16),
        in_specs=[pl.BlockSpec(memory_space=pltpu.SMEM), vm, vm, vm, vm],
        out_specs=vm,
        scratch_shapes=[pltpu.VMEM((groups, tokens // groups, columns), BF16)],
        name="pack_kv",
    )(idx, run_a, run_b, sq_a, sq_b)


def sent_kernel(
    rows_ref, q_ref, kv_ref, m_ref, l_ref, a_ref, out_ref, order_ref, m_s, l_s, a_s, wide_ref
):
    slots = kv_ref.shape[0]
    requests = q_ref.shape[0]
    for k in range(slots + WAYS):
        order_ref[k] = 0
    count = 0
    for k in range(slots):
        order_ref[count] = k
        count = count + jnp.where(rows_ref[k] >= 0, 1, 0)
    m_s[...] = m_ref[...]
    l_s[...] = l_ref[...]
    a_s[...] = a_ref[...]

    def some_slots(j, carry):
        found = []
        for u in range(WAYS):
            at = j * WAYS + u
            k = order_ref[at]
            row = jnp.maximum(rows_ref[k], 0)
            s = (
                lax.dot_general(
                    q_ref[row],
                    kv_ref[k, :, :HD],
                    (((1,), (1,)), ((), ())),
                    preferred_element_type=F32,
                )
                * INV_ROOT
            )
            top = jnp.max(s, axis=1, keepdims=True)
            w = jnp.exp(s - top)
            total = jnp.sum(w, axis=1, keepdims=True)
            acc = jnp.dot(w.astype(BF16), kv_ref[k, :, HD:], preferred_element_type=F32)
            found.append((row, jnp.where(at < count, top, -jnp.inf), total, acc))
        for row, new, total, acc in found:
            old = m_s[row]
            top = jnp.maximum(old, new)
            keep, fresh = jnp.exp(old - top), jnp.exp(new - top)
            m_s[row] = top
            l_s[row] = l_s[row] * keep + total * fresh
            a_s[row] = a_s[row] * keep + acc * fresh
        return carry

    lax.fori_loop(0, (count + WAYS - 1) // WAYS, some_slots, 0)
    for r in range(requests):
        value = a_s[r] / l_s[r]
        for h in range(value.shape[0] // NEW):
            wide_ref[r * NEW : (r + 1) * NEW, h * HD : (h + 1) * HD] = value[h * NEW : (h + 1) * NEW]
    value = wide_ref[...].astype(BF16)
    for c in range(out_ref.shape[0]):
        out_ref[c] = value


def sent_attention(rows, q, kv, m, l, acc, copies):
    slots = kv.shape[0]
    vm = pl.BlockSpec(memory_space=pltpu.VMEM)
    state = pltpu.VMEM(acc.shape, F32)
    wide = (q.shape[0] * NEW, q.shape[1] // NEW * HD)
    return pl.pallas_call(
        sent_kernel,
        out_shape=jax.ShapeDtypeStruct((copies,) + wide, BF16),
        in_specs=[pl.BlockSpec(memory_space=pltpu.SMEM), vm, vm, vm, vm, vm],
        out_specs=vm,
        scratch_shapes=[
            pltpu.SMEM((slots + WAYS,), jnp.int32),
            state,
            state,
            state,
            pltpu.VMEM(wide, F32),
        ],
        name="sent_attention",
    )(rows, q, kv, m, l, acc)


def terms_kernel(where_ref, g_ref, w_ref, *refs, steps, planes):
    outs, acc_ref = refs[:-1], refs[-1]
    owners, rows, half = g_ref.shape
    part = jnp.dot(
        g_ref[...].reshape(owners * rows, half), w_ref[0, 0], preferred_element_type=F32
    ).reshape(acc_ref.shape)

    @pl.when(pl.program_id(0) == 0)
    def _():
        acc_ref[...] = part

    @pl.when(pl.program_id(0) == 1)
    def _():
        acc_ref[...] += part
        for k, out_ref in zip(steps, outs, strict=True):
            out_ref[...] = acc_ref[lax.rem(where_ref[0] + k, planes) // 2].astype(BF16)


def terms(where, gathered, w, steps, side_block, planes):
    owners, rows, depth = gathered.shape
    columns, half, width = w.shape[1:]
    shape = jax.ShapeDtypeStruct((rows, width), BF16)

    def w_block(j, at):
        side = lax.rem(at[0] + steps[0], 2)
        d = lax.rem(2 * side + side_block - at[1] + columns, columns)
        return at[2] + j - 2 * at[2] * j, d, 0, 0

    return pl.pallas_call(
        lambda *refs: terms_kernel(*refs, steps=steps, planes=planes),
        out_shape=[shape] * len(steps),
        grid_spec=pltpu.PrefetchScalarGridSpec(
            num_scalar_prefetch=1,
            grid=(2,),
            in_specs=[
                pl.BlockSpec((owners, rows, half), lambda j, at: (0, 0, j)),
                pl.BlockSpec((1, 1, half, width), w_block),
            ],
            out_specs=[pl.BlockSpec((rows, width), lambda j, at: (0, 0))] * len(steps),
            scratch_shapes=[pltpu.VMEM((owners, rows, width), F32)],
        ),
        name="out_terms",
    )(where, gathered, w)


def shift_x(v, k):
    n = lax.axis_size("x")
    return lax.ppermute(v, "x", [(i, (i + k) % n) for i in range(n)])


def gather_w_out(w_out):
    core = lax.axis_index("grp")
    half = w_out.shape[0] // 2
    own = lax.dynamic_index_in_dim(w_out.reshape(2, half, -1), core, 0, keepdims=False)
    before, after = shift_x(own, 1), shift_x(own, -1)
    far_a, far_b = shift_x(before[: half // 2], 1), shift_x(after[half // 2 :], -1)
    mine = jnp.stack([own, after, jnp.concatenate([far_a, far_b], axis=0), before])
    other = lax.ppermute(mine, "grp", [(0, 1), (1, 0)])
    return jnp.stack([mine, other])


def add_rounded(a, b):
    return (a.astype(F32) + b.astype(F32)).astype(BF16)


def mix(gathered, w):
    planes = lax.axis_size("tp")
    me, x, core = lax.axis_index("tp"), lax.axis_index("x"), lax.axis_index("grp")
    where = jnp.stack([me, x, core]).astype(jnp.int32)
    far = planes // 2
    part, up, down = [{}, {}], [None, None], [None, None]
    for steps in (tuple(range(far, -1, -2)) + (planes - 2,), (far - 1, far + 1, 1, planes - 1)):
        for i in range(2):
            found = terms(where, gathered, w, steps, i, planes)
            part[i].update(zip(steps, found, strict=True))
            if far in steps:
                first = part[i][far]
                half = first.shape[0] // 2
                up[i], down[i] = shift_tp(first[:half], 1), shift_tp(first[half:], -1)
    for i in range(2):
        near, back = part[i][far - 1], part[i][far + 1]
        u, d = up[i], down[i]
        up[i] = shift_tp(jnp.concatenate([add_rounded(near[:half], u), near[half:]], axis=0), 1)
        down[i] = shift_tp(jnp.concatenate([back[:half], add_rounded(back[half:], d)], axis=0), -1)
    for k in range(far - 2, 0, -1):
        for i in range(2):
            up[i], down[i] = (
                shift_tp(add_rounded(part[i][k], up[i]), 1),
                shift_tp(add_rounded(part[i][planes - k], down[i]), -1),
            )
    done = [
        (part[i][0].astype(F32) + up[i].astype(F32) + down[i].astype(F32)).astype(BF16)
        for i in range(2)
    ]
    xs = lax.axis_size("x")
    got = []
    for k in range(2):
        moves = []
        for xo in range(xs):
            for t in range(planes):
                to = (2 * (t % 2) + ((xo % 2) ^ k)) * planes + 2 * (t // 2) + xo // 2
                moves.append((xo * planes + t, to))
        piece = jnp.where(x % 2 == k, done[0], done[1])
        got.append(lax.ppermute(piece, ("x", "tp"), moves))
    return jnp.where(
        x % 2 == 0, jnp.concatenate([got[0], got[1]], axis=0), jnp.concatenate([got[1], got[0]], axis=0)
    )


def own_kernel(scale_ref, length_ref, q_ref, new_ref, code_ref, m_ref, l_ref, a_ref):
    count, queries, _ = q_ref.shape
    context = code_ref.shape[1]
    place = lax.broadcasted_iota(jnp.int32, (1, context), 1)
    turn = lax.broadcasted_iota(jnp.int32, (queries, 1), 0) % NEW
    for r in range(count):
        request = pl.program_id(0) * count + r
        key_scale = jnp.zeros((1, context), F32)
        value_scale = jnp.zeros((1, context), F32)
        for b in range(context // CBLK):
            inside = place // CBLK == b
            key_scale = jnp.where(inside, scale_ref[request, 2 * b], key_scale)
            value_scale = jnp.where(inside, scale_ref[request, 2 * b + 1], value_scale)
        q = q_ref[r]
        s = lax.dot_general(
            q, code_ref[r, :, :HD], (((1,), (1,)), ((), ())), preferred_element_type=F32
        )
        s = jnp.where(place < length_ref[request], s * key_scale * INV_ROOT, -jnp.inf)
        top = jnp.max(s, axis=1, keepdims=True)
        wide = q.astype(F32)
        fresh = []
        for j in range(NEW):
            key = new_ref[r, j : j + 1, :HD].astype(F32)
            score = jnp.sum(wide * key, axis=1, keepdims=True) * INV_ROOT
            score = jnp.where(turn >= j, score, -jnp.inf)
            fresh.append(score)
            top = jnp.maximum(top, score)
        w = jnp.exp(s - top)
        total = jnp.sum(w, axis=1, keepdims=True)
        acc = jnp.dot(
            (w * value_scale).astype(BF16), code_ref[r, :, HD:], preferred_element_type=F32
        )
        for j in range(NEW):
            weight = jnp.exp(fresh[j] - top)
            total += weight
            acc += weight.astype(BF16).astype(F32) * new_ref[r, j : j + 1, HD:].astype(F32)
        m_ref[r] = jnp.broadcast_to(top, acc.shape)
        l_ref[r] = jnp.broadcast_to(total, acc.shape)
        a_ref[r] = acc


def own_attention(q, new_kv, cache_codes, scales, lengths):
    requests, queries, depth = q.shape
    count = 4
    context, columns = cache_codes.shape[1:]
    smem = pl.BlockSpec(memory_space=pltpu.SMEM)
    shape = jax.ShapeDtypeStruct((requests, queries, depth), F32)
    block = pl.BlockSpec((count, queries, depth), lambda i: (i, 0, 0))
    return pl.pallas_call(
        own_kernel,
        out_shape=[shape] * 3,
        grid=(requests // count,),
        in_specs=[
            smem,
            smem,
            block,
            pl.BlockSpec((count, NEW, columns), lambda i: (i, 0, 0)),
            pl.BlockSpec((count, context, columns), lambda i: (i, 0, 0)),
        ],
        out_specs=[block] * 3,
        name="own_attention",
    )(scales, lengths, q, new_kv, cache_codes)


def project(prompt, w_kv):
    n = lax.axis_size("tp")
    me = lax.axis_index("tp")
    tokens, part = prompt.shape
    blocks = w_kv.reshape(n, part, w_kv.shape[1])
    half = tokens // 2

    def term(piece, k):
        w = lax.dynamic_index_in_dim(blocks, (me + k) % n, 0, keepdims=False)
        wide = piece.astype(F32)
        return (
            jnp.dot(piece, w, preferred_element_type=F32),
            jnp.sum(wide * wide, axis=1, keepdims=True),
        )

    first = prompt[:half]
    second = lax.optimization_barrier((prompt, first))[0][half:]
    pieces = [first, second]
    up, down = list(pieces), list(pieces)
    sums = [None, None]
    marks = []

    def add(c, piece, k):
        run, sq = term(piece, k)
        sums[c] = (run, sq) if sums[c] is None else (sums[c][0] + run, sums[c][1] + sq)

    for step in range(1, n // 2):
        for c in range(2):
            up[c], down[c] = shift_tp(up[c], 1), shift_tp(down[c], -1)
        marks.append(up[0])
        if step == 1:
            held = lax.optimization_barrier((pieces[0], pieces[1], up[0], down[0]))
            up[0], down[0] = held[2], held[3]
            add(0, held[0], 0)
            add(1, held[1], 0)
        for c in range(2):
            add(c, up[c], -step)
            add(c, down[c], step)
    up[0], down[1] = shift_tp(up[0], 1), shift_tp(down[1], -1)
    add(0, up[0], n // 2)
    add(1, down[1], n // 2)
    return sums, marks


def on_device(
    prompt, w_kv, block_owner, block_row, queries, new_kv, cache_codes, cache_scales, lengths, w_out
):
    owners = lax.axis_size("grp") * lax.axis_size("y") * lax.axis_size("x")
    row_count = queries.shape[0]
    head_group = HQ // KVH
    features = w_kv.shape[0]
    groups = block_row.shape[0] // CAP

    sums, marks = project(prompt, w_kv)
    w = gather_w_out(lax.optimization_barrier((w_out, marks[0]))[0])
    block_owner, block_row = lax.optimization_barrier((block_owner, block_row, marks[1]))[:2]

    group_owner, group_row = block_owner[::CAP, 0], block_row[::CAP]
    hit = group_owner[None, :] == jnp.arange(owners, dtype=jnp.int32)[:, None]
    idx = jnp.sum(jnp.where(hit, jnp.arange(groups, dtype=jnp.int32)[None, :], 0), axis=1)
    send_rows = jnp.sum(jnp.where(hit, group_row[None, :] + 1, 0), axis=1) - 1
    rows = lax.all_to_all(
        jnp.broadcast_to(send_rows[:, None], (owners, 8)), ("grp", "y", "x"), 0, 0, tiled=True
    )[:, 0]

    queries = lax.optimization_barrier((queries, marks[2]))[0]
    q = queries.reshape(row_count, NEW, head_group, HD).transpose(0, 2, 1, 3)
    q = q.reshape(row_count, head_group * NEW, HD)
    scales = cache_scales.reshape(row_count, -1)

    send_kv = pack(idx, sums, owners, groups, features)
    kv = lax.all_to_all(send_kv, ("grp", "y", "x"), 0, 0, tiled=True)
    q, rows, _ = lax.optimization_barrier((q, rows, send_kv))
    m, l, acc = own_attention(q, new_kv, cache_codes, scales, lengths)
    attention = sent_attention(rows, q, kv, m, l, acc, lax.axis_size("y"))
    gathered = lax.all_to_all(attention, "y", 0, 0, tiled=True)
    return mix(gathered, w)


def solution(mesh):
    side = math.isqrt(mesh.shape["seq"])
    sizes = (mesh.shape["grp"], side, side, mesh.shape["tp"])
    mesh = jax.sharding.Mesh(mesh.devices.reshape(sizes), ("grp", "y", "x", "tp"))
    owner = ("grp", "y", "x")
    in_specs = (
        P(owner, "tp"),
        P(None, "tp"),
        P(owner, None),
        P(owner),
        P(owner, None, "tp"),
        P(owner, None, "tp"),
        P(owner, None, "tp"),
        P(owner, None, "tp"),
        P(owner),
        P("tp", ("y", "x")),
    )
    out_specs = P(("grp", "tp"), ("y", "x"))
    return jax.shard_map(
        on_device, mesh=mesh, in_specs=in_specs, out_specs=out_specs, check_vma=False
    )
```

```python
import math

import jax
import jax.numpy as jnp
from jax import lax
from jax.experimental import pallas as pl
from jax.experimental.pallas import tpu as pltpu
from jax.sharding import PartitionSpec as P


HQ = 64
KVH = 8
HD = 128
NEW = 4
CBLK = 16
CAP = 8
WAYS = 4
EPS = 1e-05
INV_ROOT = 1.0 / math.sqrt(HD)
F32 = jnp.float32
BF16 = jnp.bfloat16


def shift_tp(x, k):
    n = lax.axis_size("tp")
    return lax.ppermute(x, "tp", [(i, (i + k) % n) for i in range(n)])


def folded_squares(x):
    wide = x.astype(F32)
    total = jnp.zeros((x.shape[0], HD), F32)
    for c in range(0, x.shape[1], HD):
        total += wide[:, c : c + HD] * wide[:, c : c + HD]
    return total


def absorb_kernel(at_ref, *refs, chunks, steps, begin):
    count, blocks = len(chunks), max(steps) + 1
    pieces, ws, rest = refs[:count], refs[count : count + blocks], refs[count + blocks :]
    before, (run_ref, sq_ref) = rest[:-2], rest[-2:]
    for c in range(run_ref.shape[0]):
        mine = [i for i in range(count) if chunks[i] == c]
        run = sum(
            jnp.dot(pieces[i][...], ws[steps[i]][0], preferred_element_type=F32) for i in mine
        )
        sq = sum(folded_squares(pieces[i][...]) for i in mine)
        run_ref[c] = run if begin else before[0][c] + run
        sq_ref[c] = sq if begin else before[1][c] + sq


def absorb(at, pieces, chunks, steps, blocks, offsets, state):
    planes = blocks.shape[0]
    rows, columns = pieces[0].shape[0], blocks.shape[2]
    vm = pl.BlockSpec(memory_space=pltpu.VMEM)

    def block_at(k):
        return pl.BlockSpec((1,) + blocks.shape[1:], lambda j, at: (lax.rem(at[0] + k, planes), 0, 0))

    return pl.pallas_call(
        lambda *refs: absorb_kernel(*refs, chunks=chunks, steps=steps, begin=not state),
        out_shape=[
            jax.ShapeDtypeStruct((2, rows, columns), F32),
            jax.ShapeDtypeStruct((2, rows, HD), F32),
        ],
        grid_spec=pltpu.PrefetchScalarGridSpec(
            num_scalar_prefetch=1,
            grid=(1,),
            in_specs=[vm] * len(pieces)
            + [block_at(k % planes) for k in offsets]
            + [vm] * len(state),
            out_specs=[vm, vm],
        ),
        name="absorb",
    )(at, *pieces, *([blocks] * len(offsets)), *state)


def pack_kernel(at_ref, idx_ref, last_a, last_b, w_ref, run_ref, sq_ref, out_ref, kv_ref, *, features):
    part = kv_ref.shape[0] // 2
    for c, last in enumerate((last_a, last_b)):
        run = run_ref[c] + jnp.dot(last[...], w_ref[0], preferred_element_type=F32)
        sq = jnp.sum(sq_ref[c] + folded_squares(last[...]), axis=1, keepdims=True)
        value = (run * lax.rsqrt(sq / features + EPS)).astype(BF16)
        kv_ref[c * part : (c + 1) * part] = value.reshape((part,) + kv_ref.shape[1:])
    for o in range(out_ref.shape[0]):
        out_ref[o] = kv_ref[idx_ref[o]]


def pack(at, idx, last, blocks, state, owners, groups):
    planes, depth, columns = blocks.shape
    rows = 2 * last[0].shape[0] // groups
    vm = pl.BlockSpec(memory_space=pltpu.VMEM)
    return pl.pallas_call(
        lambda *refs: pack_kernel(*refs, features=planes * depth),
        out_shape=jax.ShapeDtypeStruct((owners, rows, columns), BF16),
        grid_spec=pltpu.PrefetchScalarGridSpec(
            num_scalar_prefetch=2,
            grid=(1,),
            in_specs=[
                vm,
                vm,
                pl.BlockSpec(
                    (1, depth, columns),
                    lambda j, at, idx: (lax.rem(at[0] + planes // 2, planes), 0, 0),
                ),
                vm,
                vm,
            ],
            out_specs=vm,
            scratch_shapes=[pltpu.VMEM((groups, rows, columns), BF16)],
        ),
        name="pack_kv",
    )(at, idx, *last, blocks, *state)


def sent_kernel(
    rows_ref, q_ref, kv_ref, m_ref, l_ref, a_ref, out_ref, order_ref, m_s, l_s, a_s, wide_ref
):
    slots = kv_ref.shape[0]
    requests = q_ref.shape[0]
    for k in range(slots + WAYS):
        order_ref[k] = 0
    count = 0
    for k in range(slots):
        order_ref[count] = k
        count = count + jnp.where(rows_ref[k] >= 0, 1, 0)
    m_s[...] = m_ref[...]
    l_s[...] = l_ref[...]
    a_s[...] = a_ref[...]

    def some_slots(j, carry):
        found = []
        for u in range(WAYS):
            at = j * WAYS + u
            k = order_ref[at]
            row = jnp.maximum(rows_ref[k], 0)
            s = (
                lax.dot_general(
                    q_ref[row],
                    kv_ref[k, :, :HD],
                    (((1,), (1,)), ((), ())),
                    preferred_element_type=F32,
                )
                * INV_ROOT
            )
            top = jnp.max(s, axis=1, keepdims=True)
            w = jnp.exp(s - top)
            total = jnp.sum(w, axis=1, keepdims=True)
            acc = jnp.dot(w.astype(BF16), kv_ref[k, :, HD:], preferred_element_type=F32)
            found.append((row, jnp.where(at < count, top, -jnp.inf), total, acc))
        for row, new, total, acc in found:
            old = m_s[row]
            top = jnp.maximum(old, new)
            keep, fresh = jnp.exp(old - top), jnp.exp(new - top)
            m_s[row] = top
            l_s[row] = l_s[row] * keep + total * fresh
            a_s[row] = a_s[row] * keep + acc * fresh
        return carry

    lax.fori_loop(0, (count + WAYS - 1) // WAYS, some_slots, 0)
    for r in range(requests):
        value = a_s[r] / l_s[r]
        for h in range(value.shape[0] // NEW):
            wide_ref[r * NEW : (r + 1) * NEW, h * HD : (h + 1) * HD] = value[h * NEW : (h + 1) * NEW]
    value = wide_ref[...].astype(BF16)
    for c in range(out_ref.shape[0]):
        out_ref[c] = value


def sent_attention(rows, q, kv, m, l, acc, copies):
    slots = kv.shape[0]
    vm = pl.BlockSpec(memory_space=pltpu.VMEM)
    state = pltpu.VMEM(acc.shape, F32)
    wide = (q.shape[0] * NEW, q.shape[1] // NEW * HD)
    return pl.pallas_call(
        sent_kernel,
        out_shape=jax.ShapeDtypeStruct((copies,) + wide, BF16),
        in_specs=[pl.BlockSpec(memory_space=pltpu.SMEM), vm, vm, vm, vm, vm],
        out_specs=vm,
        scratch_shapes=[
            pltpu.SMEM((slots + WAYS,), jnp.int32),
            state,
            state,
            state,
            pltpu.VMEM(wide, F32),
        ],
        name="sent_attention",
    )(rows, q, kv, m, l, acc)


def terms_kernel(where_ref, g_ref, w_ref, *outs, steps, planes):
    owners, rows, depth = g_ref.shape
    width = w_ref.shape[2]
    acc_ref = outs[-1]
    acc_ref[...] = jnp.dot(
        g_ref[...].reshape(owners * rows, depth), w_ref[0], preferred_element_type=F32
    ).reshape(acc_ref.shape)
    i = pl.program_id(0)
    columns = pl.ds(pl.multiple_of(i * width, width), width)
    at = 0
    for k in steps:
        value = acc_ref[lax.rem(where_ref[0] + k, planes) // 2].astype(BF16)
        if k == planes // 2:
            outs[0][:, columns] = value[: rows // 2]
            outs[1][:, columns] = value[rows // 2 :]
            at = 2
        else:
            outs[at][:, columns] = value
            at += 1


def terms(where, gathered, w, steps, planes):
    owners, rows, depth = gathered.shape
    columns, _, width = w.shape

    def w_block(i, at):
        side = lax.rem(at[0] + steps[0], 2)
        return lax.rem(2 * side + i - at[1] + columns, columns), 0, 0

    heights = []
    for k in steps:
        heights += [rows // 2] * 2 if k == planes // 2 else [rows]
    return pl.pallas_call(
        lambda *refs: terms_kernel(*refs, steps=steps, planes=planes),
        out_shape=[jax.ShapeDtypeStruct((h, 2 * width), BF16) for h in heights],
        grid_spec=pltpu.PrefetchScalarGridSpec(
            num_scalar_prefetch=1,
            grid=(2,),
            in_specs=[
                pl.BlockSpec((owners, rows, depth), lambda i, at: (0, 0, 0)),
                pl.BlockSpec((1, depth, width), w_block),
            ],
            out_specs=[pl.BlockSpec((h, 2 * width), lambda i, at: (0, 0)) for h in heights],
            scratch_shapes=[pltpu.VMEM((owners, rows, width), F32)],
        ),
        name="out_terms",
    )(where, gathered, w)


def add_kernel(near_ref, back_ref, up_ref, down_ref, a_ref, b_ref):
    rows, come = near_ref.shape[0], up_ref.shape[0]
    a_ref[:come] = (near_ref[:come].astype(F32) + up_ref[...].astype(F32)).astype(BF16)
    b_ref[rows - come :] = (
        back_ref[rows - come :].astype(F32) + down_ref[...].astype(F32)
    ).astype(BF16)
    if come < rows:
        a_ref[come:] = near_ref[come:]
        b_ref[: rows - come] = back_ref[: rows - come]


def add_both(near, back, up, down):
    vm = pl.BlockSpec(memory_space=pltpu.VMEM)
    shape = jax.ShapeDtypeStruct(near.shape, BF16)
    return pl.pallas_call(
        add_kernel, out_shape=[shape] * 2, in_specs=[vm] * 4, out_specs=[vm] * 2, name="add_terms"
    )(near, back, up, down)


def shift_x(v, k):
    n = lax.axis_size("x")
    return lax.ppermute(v, "x", [(i, (i + k) % n) for i in range(n)])


def gather_w_out(w_out):
    before = shift_x(w_out, 1)
    after = shift_x(w_out, -1)
    far = shift_x(before, 1)
    return jnp.stack([w_out, after, far, before])


def mix(where, gathered, w):
    planes = lax.axis_size("tp")
    x = lax.axis_index("x")
    far = planes // 2
    even = tuple(range(far, -1, -2)) + (planes - 2,)
    odd = (far - 1, far + 1, 1, planes - 1)
    up, down, *found = terms(where, gathered, w, even, planes)
    part = dict(zip(even[1:], found, strict=True))
    up, down = shift_tp(up, 1), shift_tp(down, -1)
    part.update(zip(odd, terms(where, gathered, w, odd, planes), strict=True))
    for k in range(far - 1, 0, -1):
        up, down = add_both(part[k], part[planes - k], up, down)
        up, down = shift_tp(up, 1), shift_tp(down, -1)
    done = (part[0].astype(F32) + up.astype(F32) + down.astype(F32)).astype(BF16)
    width = done.shape[1] // 2
    xs = lax.axis_size("x")
    got = []
    for k in range(2):
        moves = []
        for xo in range(xs):
            for t in range(planes):
                to = (2 * (t % 2) + ((xo % 2) ^ k)) * planes + 2 * (t // 2) + xo // 2
                moves.append((xo * planes + t, to))
        piece = jnp.where(x % 2 == k, done[:, :width], done[:, width:])
        got.append(lax.ppermute(piece, ("x", "tp"), moves))
    return jnp.where(
        x % 2 == 0, jnp.concatenate([got[0], got[1]], axis=0), jnp.concatenate([got[1], got[0]], axis=0)
    )


def own_kernel(scale_ref, length_ref, q_ref, new_ref, code_ref, m_ref, l_ref, a_ref):
    count, queries, _ = q_ref.shape
    context = code_ref.shape[1]
    place = lax.broadcasted_iota(jnp.int32, (1, context), 1)
    turn = lax.broadcasted_iota(jnp.int32, (queries, 1), 0) % NEW
    for r in range(count):
        request = pl.program_id(0) * count + r
        key_scale = jnp.zeros((1, context), F32)
        value_scale = jnp.zeros((1, context), F32)
        for b in range(context // CBLK):
            inside = place // CBLK == b
            key_scale = jnp.where(inside, scale_ref[request, 2 * b], key_scale)
            value_scale = jnp.where(inside, scale_ref[request, 2 * b + 1], value_scale)
        q = q_ref[r]
        s = lax.dot_general(
            q, code_ref[r, :, :HD], (((1,), (1,)), ((), ())), preferred_element_type=F32
        )
        s = jnp.where(place < length_ref[request], s * key_scale * INV_ROOT, -jnp.inf)
        top = jnp.max(s, axis=1, keepdims=True)
        wide = q.astype(F32)
        fresh = []
        for j in range(NEW):
            key = new_ref[r, j : j + 1, :HD].astype(F32)
            score = jnp.sum(wide * key, axis=1, keepdims=True) * INV_ROOT
            score = jnp.where(turn >= j, score, -jnp.inf)
            fresh.append(score)
            top = jnp.maximum(top, score)
        w = jnp.exp(s - top)
        total = jnp.sum(w, axis=1, keepdims=True)
        acc = jnp.dot(
            (w * value_scale).astype(BF16), code_ref[r, :, HD:], preferred_element_type=F32
        )
        for j in range(NEW):
            weight = jnp.exp(fresh[j] - top)
            total += weight
            acc += weight.astype(BF16).astype(F32) * new_ref[r, j : j + 1, HD:].astype(F32)
        m_ref[r] = jnp.broadcast_to(top, acc.shape)
        l_ref[r] = jnp.broadcast_to(total, acc.shape)
        a_ref[r] = acc


def own_attention(q, new_kv, cache_codes, scales, lengths):
    requests, queries, depth = q.shape
    count = 4
    context, columns = cache_codes.shape[1:]
    smem = pl.BlockSpec(memory_space=pltpu.SMEM)
    shape = jax.ShapeDtypeStruct((requests, queries, depth), F32)
    block = pl.BlockSpec((count, queries, depth), lambda i: (i, 0, 0))
    return pl.pallas_call(
        own_kernel,
        out_shape=[shape] * 3,
        grid=(requests // count,),
        in_specs=[
            smem,
            smem,
            block,
            pl.BlockSpec((count, NEW, columns), lambda i: (i, 0, 0)),
            pl.BlockSpec((count, context, columns), lambda i: (i, 0, 0)),
        ],
        out_specs=[block] * 3,
        name="own_attention",
    )(scales, lengths, q, new_kv, cache_codes)


def project(where, first, second, blocks):
    n = lax.axis_size("tp")
    up, down = [first, second], [first, second]
    pieces, chunks, steps, offsets = [first, second], (0, 1), (0, 0), [0]
    state, marks = (), []
    for step in range(1, n // 2):
        for c in range(2):
            up[c] = shift_tp(up[c], 1)
            down[c] = shift_tp(down[c], -1)
        marks.append(up[0])
        i = len(offsets)
        pieces += [up[0], down[0], up[1], down[1]]
        chunks, steps = chunks + (0, 0, 1, 1), steps + (i, i + 1, i, i + 1)
        state = absorb(where, pieces, chunks, steps, blocks, offsets + [-step, step], state)
        pieces, chunks, steps, offsets = [], (), (), []
    last_up = shift_tp(up[0], 1)
    last_down = shift_tp(down[1], -1)
    return (last_up, last_down), state, marks


def on_device(
    prompt, w_kv, block_owner, block_row, queries, new_kv, cache_codes, cache_scales, lengths, w_out
):
    owners = lax.axis_size("grp") * lax.axis_size("y") * lax.axis_size("x")
    planes = lax.axis_size("tp")
    row_count = queries.shape[0]
    head_group = HQ // KVH
    groups = block_row.shape[0] // CAP
    where = jnp.stack([lax.axis_index("tp"), lax.axis_index("x")]).astype(jnp.int32)

    tokens, depth = prompt.shape
    blocks = w_kv.reshape(planes, depth, w_kv.shape[1])
    first = prompt[: tokens // 2]
    second = lax.optimization_barrier((prompt, first))[0][tokens // 2 :]

    block_owner, block_row = lax.optimization_barrier((block_owner, block_row, second))[:2]
    group_owner, group_row = block_owner[::CAP, 0], block_row[::CAP]
    hit = group_owner[None, :] == jnp.arange(owners, dtype=jnp.int32)[:, None]
    idx = jnp.sum(jnp.where(hit, jnp.arange(groups, dtype=jnp.int32)[None, :], 0), axis=1)
    send_rows = jnp.sum(jnp.where(hit, group_row[None, :] + 1, 0), axis=1) - 1
    send_rows = jnp.broadcast_to(send_rows[:, None], (owners, 8))
    rows = lax.all_to_all(send_rows, ("grp", "y", "x"), 0, 0, tiled=True)
    rows = rows[:, 0]

    last, state, marks = project(where, first, second, blocks)
    w = gather_w_out(lax.optimization_barrier((w_out, marks[0]))[0])

    queries = lax.optimization_barrier((queries, marks[2]))[0]
    q = queries.reshape(row_count, NEW, head_group, HD).transpose(0, 2, 1, 3)
    q = q.reshape(row_count, head_group * NEW, HD)
    scales = cache_scales.reshape(row_count, -1)

    send_kv = pack(where, idx, last, blocks, state, owners, groups)
    kv = lax.all_to_all(send_kv, ("grp", "y", "x"), 0, 0, tiled=True)
    q, rows, _ = lax.optimization_barrier((q, rows, send_kv))
    m, l, acc = own_attention(q, new_kv, cache_codes, scales, lengths)
    attention = sent_attention(rows, q, kv, m, l, acc, lax.axis_size("y"))
    gathered = lax.all_to_all(attention, "y", 0, 0, tiled=True)
    return mix(where, gathered, w)


def solution(mesh):
    side = math.isqrt(mesh.shape["seq"])
    sizes = (mesh.shape["grp"], side, side, mesh.shape["tp"])
    mesh = jax.sharding.Mesh(mesh.devices.reshape(sizes), ("grp", "y", "x", "tp"))
    owner = ("grp", "y", "x")
    in_specs = (
        P(owner, "tp"),
        P(None, "tp"),
        P(owner, None),
        P(owner),
        P(owner, None, "tp"),
        P(owner, None, "tp"),
        P(owner, None, "tp"),
        P(owner, None, "tp"),
        P(owner),
        P("tp", ("y", "x")),
    )
    out_specs = P(("grp", "tp"), ("y", "x"))

    return jax.shard_map(
        on_device, mesh=mesh, in_specs=in_specs, out_specs=out_specs, check_vma=False
    )
```
